32 devices in a mesh: parts: 1, chan: 16 (over z, y, core), tm: 2 (over x), freq: 1.
Axes of the slice: x: 2, y: 2, z: 4, core: 2. Of those that a mesh axis runs over, the one named last changes fastest.
Arguments:
- spectra: bfloat16 [2, 512, 16, 2048], P(None, 'freq', 'tm', ('parts', 'chan')), may hold values from -6 to 6
- owners: int32 [4], P('parts'), may hold values from 0 to 15
- source_rows: int32 [4, 16], P('parts'), may hold values from 0 to 127
Outputs:
- correlations: float32 [4, 16, 2048, 128], P(None, ('tm', 'freq'), ('parts', 'chan'))
The draws below stay inside these ranges and needn't reach their ends.
All inputs are finite; a program needn't handle non-finite values.
Results may differ from the reference program's by a relative error of at most 0.0037.
Values may be sent and summed in bfloat16 or wider, within the bound.
A program may use at most 64 MiB of HBM per device.

```python
import jax
import jax.numpy as jnp
from jax import lax

FREQ_BINS = 512
WINDOW_LEN = 4096
FIRST_BIN = 64
SOURCES = 16
LAGS = 128
STEPS = 4
C_DEV = 128
CHANNELS = 2048
WINDOWS = 16
SHARDS = 16
N_CHAN = 16


def place_ends(result, key, low, top_value):
    spot = [jax.random.randint(jax.random.fold_in(key, axis), (), 0, length) for axis, length in enumerate(result.shape)]
    main_axis = result.shape.index(max(result.shape))
    next_to = spot[:main_axis] + [(spot[main_axis] + 1) % result.shape[main_axis]] + spot[main_axis + 1:]
    return result.at[tuple(spot)].set(low).at[tuple(next_to)].set(top_value)


def shard_levels(own_key, dims, pieces, smallest, top_value):
    def one(position, parts):
        steps = jax.random.uniform(jax.random.fold_in(jax.random.fold_in(own_key, 6), position), (parts,), jnp.float32, smallest / len(pieces), top_value / len(pieces))
        return jnp.repeat(jnp.exp(steps), dims[position] // parts).reshape((-1,) + (1,) * (len(dims) - position - 1))

    factor_of = one(*pieces[0])
    for cut in pieces[1:]:
        factor_of = factor_of * one(*cut)
    return factor_of


def gaussian(key, extent, width, reach, shards=(), held_as=jnp.bfloat16):
    loudness = shard_levels(key, extent, shards, -0.22, 0.18) if shards else 1.0
    drawn = jax.random.normal(key, extent, jnp.float32) * width * loudness
    return jnp.minimum(jnp.maximum(drawn, -reach), reach).astype(held_as)


def setup_inputs(seed: int = 0, part: int = 0) -> dict:
    streams_of = jax.random.split(jax.random.key(seed), 4)
    part_splits = jax.random.split(jax.random.fold_in(streams_of[3], part), 4)
    return {
        "spectra": gaussian(part_splits[0], (2, FREQ_BINS, WINDOWS, CHANNELS), 1.0, 6.0, ((2, 2), (3, 16))),
        "owners": place_ends(jax.random.randint(part_splits[1], (STEPS,), 0, SHARDS), jax.random.fold_in(part_splits[1], 1), 0, SHARDS - 1).astype(jnp.int32),
        "source_rows": place_ends(jax.random.randint(part_splits[2], (STEPS, SOURCES), 0, C_DEV), jax.random.fold_in(part_splits[2], 1), 0, C_DEV - 1).astype(jnp.int32),
    }


WATER = 0.5

def whiten(block):
    values = block.astype(jnp.float32)
    size = jnp.sqrt(values[0] * values[0] + values[1] * values[1]) + WATER
    return (values / size[None]).astype(jnp.bfloat16)

def make_tables(first_bin, count):
    bins = first_bin + jnp.arange(count, dtype=jnp.int32)
    shifts = jnp.arange(LAGS, dtype=jnp.int32) - LAGS // 2
    phase = jnp.mod(bins[:, None] * shifts[None, :], WINDOW_LEN).astype(jnp.float32)
    angle = phase * (2.0 * 3.141592653589793 / WINDOW_LEN)
    return (jnp.cos(angle), jnp.sin(angle))

def reference(spectra, owners, source_rows):
    chosen = (owners[:, None] * C_DEV + source_rows).reshape(-1).astype(jnp.int32)
    picked = whiten(jnp.take(spectra, chosen, axis=3))
    picked = picked.reshape(2, FREQ_BINS, WINDOWS, STEPS, SOURCES).astype(jnp.float32)
    picked = jnp.transpose(picked, (3, 0, 1, 2, 4))
    flipped = jnp.stack([picked, jnp.stack([-picked[:, 1], picked[:, 0]], axis=1)], axis=1)
    cosine, sine = make_tables(FIRST_BIN, FREQ_BINS)
    hp = lax.Precision.HIGHEST

    def shard_lags(index):
        start = (index * C_DEV).astype(jnp.int32)
        local = lax.dynamic_slice_in_dim(spectra, start, C_DEV, 3)
        local = whiten(local).astype(jnp.float32)
        cross = jnp.einsum('tokfws,kfwc->tofsc', flipped, local, precision=hp)
        lags = jnp.einsum('tfsc,fl->tscl', cross[:, 0], cosine, precision=hp)
        lags = lags - jnp.einsum('tfsc,fl->tscl', cross[:, 1], sine, precision=hp)
        return lags / WINDOWS
    every = lax.map(shard_lags, jnp.arange(N_CHAN, dtype=jnp.int32))
    every = jnp.transpose(every, (1, 2, 0, 3, 4))
    return every.reshape(STEPS, SOURCES, CHANNELS, LAGS)
```

```python
import jax
import jax.numpy as jnp
from jax import lax
from jax.sharding import PartitionSpec as P

WINDOW_LEN = 4096
FIRST_BIN = 64
LAGS = 128
WATER = 0.5


def whiten(block):
    values = block.astype(jnp.float32)
    size = jnp.sqrt(values[0] * values[0] + values[1] * values[1]) + WATER
    return (values / size[None]).astype(jnp.bfloat16)


def make_tables(first_bin, count):
    bins = first_bin + jnp.arange(count, dtype=jnp.int32)
    shifts = jnp.arange(LAGS, dtype=jnp.int32) - LAGS // 2
    phase = jnp.mod(bins[:, None] * shifts[None, :], WINDOW_LEN).astype(jnp.float32)
    angle = phase * (2.0 * 3.141592653589793 / WINDOW_LEN)
    return jnp.stack([jnp.cos(angle), -jnp.sin(angle)])


def per_device(spectra, owners, source_rows):
    whitened = whiten(spectra)
    bins, wins, chans = whitened.shape[1:]
    steps, per_step = source_rows.shape
    total = steps * per_step
    scale = 1.0 / (wins * lax.axis_size("tm"))
    first_bin = FIRST_BIN + lax.axis_index("freq") * bins
    tables = (make_tables(first_bin, bins) * scale).astype(jnp.bfloat16)
    mine = owners == lax.axis_index("chan")
    rows = jnp.where(mine[:, None], source_rows, -1).reshape(total)
    pick = (rows[:, None] == jnp.arange(chans)[None, :]).astype(jnp.bfloat16)
    block = jnp.einsum("kfwc,sc->kfsw", whitened, pick, preferred_element_type=jnp.bfloat16)
    block = lax.psum(block, "chan")
    flipped = jnp.stack([block, jnp.stack([-block[1], block[0]])])
    cross = jnp.einsum("okfsw,kfwc->ofsc", flipped, whitened, preferred_element_type=jnp.float32)
    cross = cross.astype(jnp.bfloat16)
    lags = jnp.einsum("ofsc,ofl->scl", cross, tables, preferred_element_type=jnp.float32)
    lags = lags.astype(jnp.bfloat16).reshape(steps, per_step, chans, LAGS)
    lags = lax.psum_scatter(lags, ("tm", "freq"), scatter_dimension=1, tiled=True)
    return lags.astype(jnp.float32)


def solution(mesh):
    placed = (P(None, "freq", "tm", ("parts", "chan")), P("parts"), P("parts", None))
    return jax.shard_map(
        per_device,
        mesh=mesh,
        in_specs=placed,
        out_specs=P(None, ("tm", "freq"), ("parts", "chan"), None),
        check_vma=False,
    )
```

```python
import functools

import jax
import jax.numpy as jnp
import numpy as np
from jax import lax
from jax.experimental import pallas as pl
from jax.experimental.pallas import tpu as pltpu
from jax.sharding import PartitionSpec as P

WINDOW_LEN = 4096
FIRST_BIN = 64
LAGS = 128
WATER = 0.5
AXES = ("parts", "chan", "tm", "freq")
MESH = pl.DeviceIdType.MESH


def table(count, scale):
    bins = FIRST_BIN + np.arange(count)
    shifts = np.arange(LAGS) - LAGS // 2
    angle = np.mod(shifts[:, None] * bins[None, :], WINDOW_LEN) * (2.0 * np.pi / WINDOW_LEN)
    return np.stack([np.cos(angle), -np.sin(angle)], axis=1) * scale


def kernel(sizes, spec_ref, pick_ref, table_ref, out_ref,
           wh, held, got1, got2, got_full, whole, cross, own, send, recv,
           bsend, brecv, xsend, xrecv):
    steps, per_step, bins, wins, chans, n_chan, n_tm, n_freq = sizes
    group = 128 // wins
    lanes = bins * wins
    half = lanes // 2
    peers = n_tm * n_freq
    per = per_step // peers
    part, me = lax.axis_index("parts"), lax.axis_index("chan")
    tm, fq = lax.axis_index("tm"), lax.axis_index("freq")
    rank = tm * n_freq + fq
    bit0, bit1 = me % 2, (me // 2) % 2
    dists = []
    while 2 ** len(dists) < n_chan:
        dists.append(2 ** len(dists))
    far = dists[2:]
    stages = [1, 2] + far + [2, 1]

    def along(d):
        return (part, me + d * (1 - 2 * ((me // d) % 2)), tm, fq)

    def peer(p):
        other = (rank + p) % peers
        return (part, me, other // n_freq, other % n_freq), other

    barrier = pltpu.get_barrier_semaphore()
    for d in dists:
        pl.semaphore_signal(barrier, inc=1, device_id=along(d), device_id_type=MESH)
    for p in range(1, peers):
        pl.semaphore_signal(barrier, inc=1, device_id=peer(p)[0], device_id_type=MESH)

    rows = 256

    def whiten(i, carry):
        at = pl.ds(pl.multiple_of(i * rows, rows), rows)
        re = spec_ref[0, at, :].astype(jnp.float32)
        im = spec_ref[1, at, :].astype(jnp.float32)
        size = jnp.sqrt(re * re + im * im) + WATER
        wh[0, at, :] = (re / size).astype(jnp.bfloat16)
        wh[1, at, :] = (im / size).astype(jnp.bfloat16)
        return carry

    lax.fori_loop(0, lanes // rows, whiten, 0)

    for k in range(2):
        for h in range(2):
            def choose(i, carry):
                at = pl.ds(pl.multiple_of(h * half + i * rows, rows), rows)
                got = lax.dot_general(pick_ref[...], wh[k, at, :], (((1,), (1,)), ((), ())),
                                      preferred_element_type=jnp.float32).astype(jnp.bfloat16)
                to = pl.ds(pl.multiple_of(i * rows, rows), rows)
                for t in range(steps):
                    held[t, 2 * k + h, :, to] = got[t * per_step:(t + 1) * per_step]
                return carry

            lax.fori_loop(0, half // rows, choose, 0)

    pl.semaphore_wait(barrier, len(dists) + peers - 1)

    keep = 2 * bit0 + bit1
    last = len(stages) - 1

    def copy(t, st):
        d = stages[st]
        if st == 0:
            src, dst = held.at[t, pl.ds(2 * (1 - bit0), 2)], got1.at[t]
        elif st == 1:
            src, dst = held.at[t, 2 * bit0 + 1 - bit1], got2.at[t]
        elif st < last - 1:
            src, dst = held.at[t, keep], got_full.at[t, st - 2]
        elif st == last - 1:
            src = dst = whole.at[t, keep]
        else:
            src = dst = whole.at[t, pl.ds(2 * bit0, 2)]
        return pltpu.make_async_remote_copy(
            src_ref=src, dst_ref=dst, send_sem=bsend.at[t, st], recv_sem=brecv.at[t, st],
            device_id=along(d), device_id_type=MESH)

    def finish(t, st):
        copy(t, st).wait()
        if st == 0:
            for q in range(2):
                held[t, 2 * bit0 + q] = held[t, 2 * bit0 + q] + got1[t, q]
        elif st == 1:
            held[t, keep] = held[t, keep] + got2[t]
        elif st < last - 1:
            held[t, keep] = held[t, keep] + got_full[t, st - 2]
        if st == last - 2:
            whole[t, keep] = held[t, keep]

    lane = lax.broadcasted_iota(jnp.int32, (1, group, 128), 2)
    bin_of = lax.broadcasted_iota(jnp.int32, (1, group, 128), 1)
    mine = (lane // wins) == bin_of

    def spread(x):
        wide = jnp.where(mine, x[:, None, :], 0.0)
        return wide.reshape(per_step * group, 128).astype(jnp.bfloat16)

    def exchange(t, p):
        return pltpu.make_async_remote_copy(
            src_ref=send.at[t, p - 1], dst_ref=recv.at[t, p - 1],
            send_sem=xsend.at[t, p - 1], recv_sem=xrecv.at[t, p - 1],
            device_id=peer(p)[0], device_id_type=MESH)

    def compute(t):
        for h in range(2):
            def one(i, carry):
                g = pl.multiple_of(i * 128, 128)
                re = whole[t, h, :, pl.ds(g, 128)].astype(jnp.float32)
                im = whole[t, 2 + h, :, pl.ds(g, 128)].astype(jnp.float32)
                wre, wim = spread(re), spread(im)
                at = pl.ds(pl.multiple_of(h * half + i * 128, 128), 128)
                right = jnp.concatenate([wh[0, at, :], wh[1, at, :]], axis=0)
                real = jnp.dot(jnp.concatenate([wre, wim], axis=1), right, preferred_element_type=jnp.float32)
                imag = jnp.dot(jnp.concatenate([-wim, wre], axis=1), right, preferred_element_type=jnp.float32)
                first = h * (bins // 2) + i * group
                for o, value in enumerate((real, imag)):
                    to = pl.ds(pl.multiple_of(o * bins + first, group), group)
                    cross[:, to, :] = value.reshape(per_step, group, chans).astype(jnp.bfloat16)
                return carry

            lax.fori_loop(0, half // 128, one, 0)

        def lag_pair(s):
            both = jnp.concatenate([cross[s], cross[s + 1]], axis=1)
            return jnp.dot(table_ref[...], both, preferred_element_type=jnp.float32)

        for p in range(1, peers):
            other = peer(p)[1]

            def away(i, carry):
                got = lag_pair(other * per + 2 * i).astype(jnp.bfloat16)
                send[t, p - 1, 2 * i] = got[:, :chans]
                send[t, p - 1, 2 * i + 1] = got[:, chans:]
                return carry

            lax.fori_loop(0, per // 2, away, 0)
            exchange(t, p).start()

        def home(i, carry):
            got = lag_pair(rank * per + 2 * i)
            own[t, 2 * i] = got[:, :chans]
            own[t, 2 * i + 1] = got[:, chans:]
            return carry

        lax.fori_loop(0, per // 2, home, 0)

    def close(t):
        for p in range(1, peers):
            exchange(t, p).wait()

        def one(j, carry):
            value = own[t, j]
            for p in range(1, peers):
                value = value + recv[t, p - 1, j].astype(jnp.float32)
            out_ref[t, j] = value.T
            return carry

        lax.fori_loop(0, per, one, 0)

    count = len(stages)
    for t in range(steps):
        copy(t, 0).start()
    for wave in range(steps + count + 1):
        for t in range(steps):
            st = wave - t
            if 0 <= st < count:
                finish(t, st)
                if st + 1 < count:
                    copy(t, st + 1).start()
            elif st == count:
                compute(t)
            elif st == count + 1:
                close(t)


def per_device(spectra, owners, source_rows):
    _, bins, wins, chans = spectra.shape
    steps, per_step = source_rows.shape
    n_chan, n_tm, n_freq = (lax.axis_size(a) for a in AXES[1:])
    peers = n_tm * n_freq
    per = per_step // peers
    lanes = bins * wins
    full = jnp.asarray(table(bins * n_freq, 1.0 / (wins * n_tm)).astype(jnp.bfloat16))
    tables = lax.dynamic_slice_in_dim(full, lax.axis_index("freq") * bins, bins, 2) if n_freq > 1 else full
    tables = tables.reshape(LAGS, 2 * bins)
    mine = owners == lax.axis_index("chan")
    rows = jnp.where(mine[:, None], source_rows, -1).reshape(-1)
    pick = (rows[:, None] == jnp.arange(chans)[None, :]).astype(jnp.bfloat16)
    far = max(n_chan.bit_length() - 3, 1)
    count = n_chan.bit_length() + 1
    sizes = (steps, per_step, bins, wins, chans, n_chan, n_tm, n_freq)
    bf16, f32 = jnp.bfloat16, jnp.float32
    quarter = (per_step, lanes // 2)
    vmem = pl.BlockSpec(memory_space=pltpu.VMEM)
    return pl.pallas_call(
        functools.partial(kernel, sizes),
        out_shape=jax.ShapeDtypeStruct((steps, per, chans, LAGS), f32),
        in_specs=[vmem] * 3,
        out_specs=vmem,
        scratch_shapes=[
            pltpu.VMEM((2, lanes, chans), bf16),
            pltpu.VMEM((steps, 4) + quarter, bf16),
            pltpu.VMEM((steps, 2) + quarter, bf16),
            pltpu.VMEM((steps,) + quarter, bf16),
            pltpu.VMEM((steps, far) + quarter, bf16),
            pltpu.VMEM((steps, 4) + quarter, bf16),
            pltpu.VMEM((per_step, 2 * bins, chans), bf16),
            pltpu.VMEM((steps, per, LAGS, chans), f32),
            pltpu.VMEM((steps, peers - 1, per, LAGS, chans), bf16),
            pltpu.VMEM((steps, peers - 1, per, LAGS, chans), bf16),
            pltpu.SemaphoreType.DMA((steps, count)),
            pltpu.SemaphoreType.DMA((steps, count)),
            pltpu.SemaphoreType.DMA((steps, peers - 1)),
            pltpu.SemaphoreType.DMA((steps, peers - 1)),
        ],
        compiler_params=pltpu.CompilerParams(collective_id=0, has_side_effects=True),
    )(spectra.reshape(2, lanes, chans), pick, tables)


def solution(mesh):
    placed = (P(None, "freq", "tm", ("parts", "chan")), P("parts"), P("parts", None))
    return jax.shard_map(
        per_device,
        mesh=mesh,
        in_specs=placed,
        out_specs=P(None, ("tm", "freq"), ("parts", "chan"), None),
        check_vma=False,
    )
```

```python
import functools

import jax
import jax.numpy as jnp
import numpy as np
from jax import lax
from jax.experimental import pallas as pl
from jax.experimental.pallas import tpu as pltpu
from jax.sharding import PartitionSpec as P

WINDOW_LEN = 4096
FIRST_BIN = 64
LAGS = 128
WATER = 0.5
AXES = ("parts", "chan", "tm", "freq")
MESH = pl.DeviceIdType.MESH


def table(count, scale):
    bins = FIRST_BIN + np.arange(count)
    shifts = np.arange(LAGS) - LAGS // 2
    angle = np.mod(shifts[:, None] * bins[None, :], WINDOW_LEN) * (2.0 * np.pi / WINDOW_LEN)
    return np.stack([np.cos(angle), -np.sin(angle)], axis=1) * scale


def layout(steps, per_step, peers):
    block = steps * (per_step // peers)
    piece = max(min(per_step, block) // 2, 2)
    return block, piece, (peers - 1) * block // piece


def kernel(sizes, owner_ref, row_ref, spec_ref, table_ref, out_ref,
           pick, right, held, got1, got2, got_full, whole, cross, own, send, recv,
           bsend, brecv, xsend, xrecv):
    steps, per_step, bins, wins, chans, n_chan, n_tm, n_freq = sizes
    group = 128 // wins
    lanes = bins * wins
    half = lanes // 2
    groups = lanes // 128
    peers = n_tm * n_freq
    per = per_step // peers
    block, piece, sends = layout(steps, per_step, peers)
    part, me = lax.axis_index("parts"), lax.axis_index("chan")
    tm, fq = lax.axis_index("tm"), lax.axis_index("freq")
    rank = tm * n_freq + fq
    bit0, bit1 = me % 2, (me // 2) % 2
    dists = []
    while 2 ** len(dists) < n_chan:
        dists.append(2 ** len(dists))
    far = dists[2:]
    stages = [1, 2] + far + [2, 1]

    def along(d):
        return (part, me + d * (1 - 2 * ((me // d) % 2)), tm, fq)

    def peer(p):
        other = (rank + p) % peers
        return (part, me, other // n_freq, other % n_freq)

    barrier = pltpu.get_barrier_semaphore()
    for d in dists:
        pl.semaphore_signal(barrier, inc=1, device_id=along(d), device_id_type=MESH)
    for p in range(1, peers):
        pl.semaphore_signal(barrier, inc=1, device_id=peer(p), device_id_type=MESH)

    channel = lax.broadcasted_iota(jnp.int32, (1, chans), 1)
    for p in range(1, peers + 1):
        for t in range(steps):
            held_here = owner_ref[t] == me
            for j in range(per):
                row = jnp.where(held_here, row_ref[t, ((rank + p) % peers) * per + j], -1)
                at = (p - 1) * block + t * per + j
                pick[pl.ds(at, 1), :] = (channel == row).astype(jnp.float32)
    chosen = pick[...].astype(jnp.bfloat16)

    def prepare(h, i):
        g = h * (groups // 2) + i
        at = pl.ds(pl.multiple_of(g * 128, 128), 128)
        re = spec_ref[0, at, :].astype(jnp.float32)
        im = spec_ref[1, at, :].astype(jnp.float32)
        inverse = 1.0 / (jnp.sqrt(re * re + im * im) + WATER)
        re = (re * inverse).astype(jnp.bfloat16)
        im = (im * inverse).astype(jnp.bfloat16)
        right[g, :128, :chans] = re
        right[g, :128, chans:] = im
        right[g, 128:, :chans] = im
        right[g, 128:, chans:] = -re
        both = jnp.concatenate([re, im], axis=0)
        got = lax.dot_general(chosen, both, (((1,), (1,)), ((), ())),
                              preferred_element_type=jnp.float32).astype(jnp.bfloat16)
        to = pl.ds(pl.multiple_of(i * 128, 128), 128)
        for u in range(steps):
            for k in range(2):
                held[u, 2 * k + h, :, to] = got[u * per_step:(u + 1) * per_step, k * 128:(k + 1) * 128]

    def repeat(count, unroll, body):
        def some(i, carry):
            for r in range(unroll):
                body(i * unroll + r)
            return carry

        lax.fori_loop(0, count // unroll, some, 0)

    for h in range(2):
        repeat(groups // 2, 4, functools.partial(prepare, h))

    pl.semaphore_wait(barrier, len(dists) + peers - 1)

    keep = 2 * bit0 + bit1
    last = len(stages) - 1

    def copy(t, st):
        d = stages[st]
        if st == 0:
            src, dst = held.at[t, pl.ds(2 * (1 - bit0), 2)], got1.at[t]
        elif st == 1:
            src, dst = held.at[t, 2 * bit0 + 1 - bit1], got2.at[t]
        elif st < last - 1:
            src, dst = held.at[t, keep], got_full.at[t, st - 2]
        elif st == last - 1:
            src = dst = whole.at[t, keep]
        else:
            src = dst = whole.at[t, pl.ds(2 * bit0, 2)]
        return pltpu.make_async_remote_copy(
            src_ref=src, dst_ref=dst, send_sem=bsend.at[t, st], recv_sem=brecv.at[t, st],
            device_id=along(d), device_id_type=MESH)

    def finish(t, st):
        copy(t, st).wait()
        if st == 0:
            for q in range(2):
                held[t, 2 * bit0 + q] = held[t, 2 * bit0 + q] + got1[t, q]
        elif st == 1:
            held[t, keep] = held[t, keep] + got2[t]
        elif st < last - 1:
            held[t, keep] = held[t, keep] + got_full[t, st - 2]
        if st == last - 2:
            whole[t, keep] = held[t, keep]

    lane = lax.broadcasted_iota(jnp.int32, (1, group, 128), 2)
    bin_of = lax.broadcasted_iota(jnp.int32, (1, group, 128), 1)
    mine = (lane // wins) == bin_of

    def spread(x):
        wide = jnp.where(mine, x[:, None, :], 0.0)
        return wide.reshape(per_step * group, 128).astype(jnp.bfloat16)

    def exchange(v):
        return pltpu.make_async_remote_copy(
            src_ref=send.at[v], dst_ref=recv.at[v], send_sem=xsend.at[v], recv_sem=xrecv.at[v],
            device_id=peer(v * piece // block + 1), device_id_type=MESH)

    def multiply(u):
        for h in range(2):
            def one(i):
                g = pl.multiple_of(i * 128, 128)
                re = whole[u, h, :, pl.ds(g, 128)].astype(jnp.float32)
                im = whole[u, 2 + h, :, pl.ds(g, 128)].astype(jnp.float32)
                left = jnp.concatenate([spread(re), spread(im)], axis=1)
                got = jnp.dot(left, right[h * (groups // 2) + i], preferred_element_type=jnp.float32)
                first = h * (bins // 2) + i * group
                for o in range(2):
                    to = pl.ds(pl.multiple_of(o * bins + first, group), group)
                    value = got[:, o * chans:(o + 1) * chans]
                    cross[:, to, :] = value.reshape(per_step, group, chans).astype(jnp.bfloat16)

            repeat(groups // 2, 2, one)

    def lag_pair(s):
        both = jnp.concatenate([cross[s], cross[s + 1]], axis=1)
        return jnp.dot(table_ref[...], both, preferred_element_type=jnp.float32)

    def compute(u):
        multiply(u)
        for n in range(per_step // piece):
            v = u * (per_step // piece) + n

            def pair(i):
                got = lag_pair(n * piece + 2 * i)
                for r in range(2):
                    value = got[:, r * chans:(r + 1) * chans]
                    if v < sends:
                        send[v, 2 * i + r] = value.astype(jnp.bfloat16)
                    else:
                        own[(v - sends) * piece + 2 * i + r] = value

            repeat(piece // 2, min(2, piece // 2), pair)
            if v < sends:
                exchange(v).start()

    def close(w):
        for p in range(1, peers):
            exchange((p - 1) * (block // piece) + w).wait()

        def one(j):
            value = own[w * piece + j]
            for p in range(1, peers):
                value = value + recv[(p - 1) * (block // piece) + w, j].astype(jnp.float32)
            out_ref[w * piece + j] = value.T

        repeat(piece, 2, one)

    count = len(stages)
    for t in range(steps):
        copy(t, 0).start()
    for wave in range(steps + count):
        for t in range(steps):
            st = wave - t
            if 0 <= st < count:
                finish(t, st)
                if st + 1 < count:
                    copy(t, st + 1).start()
            elif st == count:
                compute(t)
    for w in range(block // piece):
        close(w)


def per_device(spectra, owners, source_rows):
    _, bins, wins, chans = spectra.shape
    steps, per_step = source_rows.shape
    n_chan, n_tm, n_freq = (lax.axis_size(a) for a in AXES[1:])
    peers = n_tm * n_freq
    per = per_step // peers
    lanes = bins * wins
    full = jnp.asarray(table(bins * n_freq, 1.0 / (wins * n_tm)).astype(jnp.bfloat16))
    tables = lax.dynamic_slice_in_dim(full, lax.axis_index("freq") * bins, bins, 2) if n_freq > 1 else full
    tables = tables.reshape(LAGS, 2 * bins)
    far = max(n_chan.bit_length() - 3, 1)
    count = n_chan.bit_length() + 1
    sizes = (steps, per_step, bins, wins, chans, n_chan, n_tm, n_freq)
    bf16, f32 = jnp.bfloat16, jnp.float32
    quarter = (per_step, lanes // 2)
    vmem = pl.BlockSpec(memory_space=pltpu.VMEM)
    smem = pl.BlockSpec(memory_space=pltpu.SMEM)
    block, piece, sends = layout(steps, per_step, peers)
    out = pl.pallas_call(
        functools.partial(kernel, sizes),
        out_shape=jax.ShapeDtypeStruct((block, chans, LAGS), f32),
        in_specs=[smem, smem, vmem, vmem],
        out_specs=vmem,
        scratch_shapes=[
            pltpu.VMEM((steps * per_step, chans), f32),
            pltpu.VMEM((lanes // 128, 256, 2 * chans), bf16),
            pltpu.VMEM((steps, 4) + quarter, bf16),
            pltpu.VMEM((steps, 2) + quarter, bf16),
            pltpu.VMEM((steps,) + quarter, bf16),
            pltpu.VMEM((steps, far) + quarter, bf16),
            pltpu.VMEM((steps, 4) + quarter, bf16),
            pltpu.VMEM((per_step, 2 * bins, chans), bf16),
            pltpu.VMEM((block, LAGS, chans), f32),
            pltpu.VMEM((max(sends, 1), piece, LAGS, chans), bf16),
            pltpu.VMEM((max(sends, 1), piece, LAGS, chans), bf16),
            pltpu.SemaphoreType.DMA((steps, count)),
            pltpu.SemaphoreType.DMA((steps, count)),
            pltpu.SemaphoreType.DMA((max(sends, 1),)),
            pltpu.SemaphoreType.DMA((max(sends, 1),)),
        ],
        compiler_params=pltpu.CompilerParams(collective_id=0, has_side_effects=True),
    )(owners, source_rows, spectra.reshape(2, lanes, chans), tables)
    return out.reshape(steps, per, chans, LAGS)


def solution(mesh):
    placed = (P(None, "freq", "tm", ("parts", "chan")), P("parts"), P("parts", None))
    return jax.shard_map(
        per_device,
        mesh=mesh,
        in_specs=placed,
        out_specs=P(None, ("tm", "freq"), ("parts", "chan"), None),
        check_vma=False,
    )
```

```python
import functools

import jax
import jax.numpy as jnp
import numpy as np
from jax import lax
from jax.experimental import pallas as pl
from jax.experimental.pallas import tpu as pltpu
from jax.sharding import PartitionSpec as P

WINDOW_LEN = 4096
FIRST_BIN = 64
LAGS = 128
WATER = 0.5
AXES = ("parts", "chan", "tm", "freq")
MESH = pl.DeviceIdType.MESH


def table(count, scale):
    bins = FIRST_BIN + np.arange(count)
    shifts = np.arange(LAGS) - LAGS // 2
    angle = np.mod(shifts[:, None] * bins[None, :], WINDOW_LEN) * (2.0 * np.pi / WINDOW_LEN)
    return np.stack([np.cos(angle), -np.sin(angle)], axis=1) * scale


def layout(steps, per_step, peers):
    block = steps * (per_step // peers)
    piece = max(min(per_step, block) // 2, 2)
    return block, piece, (peers - 1) * block // piece


def kernel(sizes, owner_ref, row_ref, spec_ref, table_ref, out_ref,
           pick, right, held, got1, got2, got_full, whole, cross, own, send, recv,
           bsend, brecv, xsend, xrecv):
    steps, per_step, bins, wins, chans, n_chan, n_tm, n_freq = sizes
    group = 128 // wins
    lanes = bins * wins
    half = lanes // 2
    groups = lanes // 128
    peers = n_tm * n_freq
    per = per_step // peers
    block, piece, sends = layout(steps, per_step, peers)
    part, me = lax.axis_index("parts"), lax.axis_index("chan")
    tm, fq = lax.axis_index("tm"), lax.axis_index("freq")
    rank = tm * n_freq + fq
    bit0, bit1 = me % 2, (me // 2) % 2
    dists = []
    while 2 ** len(dists) < n_chan:
        dists.append(2 ** len(dists))
    far = dists[2:]
    stages = [1, 2] + far + [2, 1]

    def along(d):
        return (part, me + d * (1 - 2 * ((me // d) % 2)), tm, fq)

    def peer(p):
        other = (rank + p) % peers
        return (part, me, other // n_freq, other % n_freq)

    barrier = pltpu.get_barrier_semaphore()
    for d in dists:
        pl.semaphore_signal(barrier, inc=1, device_id=along(d), device_id_type=MESH)
    for p in range(1, peers):
        pl.semaphore_signal(barrier, inc=1, device_id=peer(p), device_id_type=MESH)

    channel = lax.broadcasted_iota(jnp.int32, (1, chans), 1)
    for p in range(1, peers + 1):
        for t in range(steps):
            held_here = owner_ref[t] == me
            for j in range(per):
                row = jnp.where(held_here, row_ref[t, ((rank + p) % peers) * per + j], -1)
                at = (p - 1) * block + t * per + j
                pick[pl.ds(at, 1), :] = (channel == row).astype(jnp.float32)
    chosen = pick[...].astype(jnp.bfloat16)

    def prepare(h, i):
        g = h * (groups // 2) + i
        at = pl.ds(pl.multiple_of(g * 128, 128), 128)
        re = spec_ref[0, at, :].astype(jnp.float32)
        im = spec_ref[1, at, :].astype(jnp.float32)
        inverse = 1.0 / (jnp.sqrt(re * re + im * im) + WATER)
        re = (re * inverse).astype(jnp.bfloat16)
        im = (im * inverse).astype(jnp.bfloat16)
        right[g, :128, :chans] = re
        right[g, :128, chans:] = im
        right[g, 128:, :chans] = im
        right[g, 128:, chans:] = -re
        both = jnp.concatenate([re, im], axis=0)
        got = lax.dot_general(chosen, both, (((1,), (1,)), ((), ())),
                              preferred_element_type=jnp.float32).astype(jnp.bfloat16)
        to = pl.ds(pl.multiple_of(i * 128, 128), 128)
        for u in range(steps):
            for k in range(2):
                held[u, 2 * k + h, :, to] = got[u * per_step:(u + 1) * per_step, k * 128:(k + 1) * 128]

    def repeat(count, unroll, body):
        def some(i, carry):
            for r in range(unroll):
                body(i * unroll + r)
            return carry

        lax.fori_loop(0, count // unroll, some, 0)

    for h in range(2):
        repeat(groups // 2, 4, functools.partial(prepare, h))

    pl.semaphore_wait(barrier, len(dists) + peers - 1)

    keep = 2 * bit0 + bit1
    last = len(stages) - 1

    def copy(t, st):
        d = stages[st]
        if st == 0:
            src, dst = held.at[t, pl.ds(2 * (1 - bit0), 2)], got1.at[t]
        elif st == 1:
            src, dst = held.at[t, 2 * bit0 + 1 - bit1], got2.at[t]
        elif st < last - 1:
            src, dst = held.at[t, keep], got_full.at[t, st - 2]
        elif st == last - 1:
            src = dst = whole.at[t, keep]
        else:
            src = dst = whole.at[t, pl.ds(2 * bit0, 2)]
        return pltpu.make_async_remote_copy(
            src_ref=src, dst_ref=dst, send_sem=bsend.at[t, st], recv_sem=brecv.at[t, st],
            device_id=along(d), device_id_type=MESH)

    def finish(t, st):
        copy(t, st).wait()
        if st == 0:
            for q in range(2):
                held[t, 2 * bit0 + q] = held[t, 2 * bit0 + q] + got1[t, q]
        elif st == 1:
            held[t, keep] = held[t, keep] + got2[t]
        elif st < last - 1:
            held[t, keep] = held[t, keep] + got_full[t, st - 2]
        if st == last - 2:
            whole[t, keep] = held[t, keep]

    lane = lax.broadcasted_iota(jnp.int32, (1, group, 128), 2)
    bin_of = lax.broadcasted_iota(jnp.int32, (1, group, 128), 1)
    mine = (lane // wins) == bin_of

    def spread(x):
        wide = jnp.where(mine, x[:, None, :], 0.0)
        return wide.reshape(per_step * group, 128).astype(jnp.bfloat16)

    def exchange(v):
        return pltpu.make_async_remote_copy(
            src_ref=send.at[v], dst_ref=recv.at[v], send_sem=xsend.at[v], recv_sem=xrecv.at[v],
            device_id=peer(v * piece // block + 1), device_id_type=MESH)

    def multiply(u, h):
        def one(i):
            g = pl.multiple_of(i * 128, 128)
            re = whole[u, h, :, pl.ds(g, 128)].astype(jnp.float32)
            im = whole[u, 2 + h, :, pl.ds(g, 128)].astype(jnp.float32)
            left = jnp.concatenate([spread(re), spread(im)], axis=1)
            got = jnp.dot(left, right[h * (groups // 2) + i], preferred_element_type=jnp.float32)
            first = h * (bins // 2) + i * group
            for o in range(2):
                to = pl.ds(pl.multiple_of(o * bins + first, group), group)
                value = got[:, o * chans:(o + 1) * chans]
                cross[:, to, :] = value.reshape(per_step, group, chans).astype(jnp.bfloat16)

        repeat(groups // 2, 2, one)

    def lag_pair(s):
        both = jnp.concatenate([cross[s], cross[s + 1]], axis=1)
        return jnp.dot(table_ref[...], both, preferred_element_type=jnp.float32)

    def compute(u, part_of):
        if part_of < 2:
            multiply(u, part_of)
        else:
            n = part_of - 2
            v = u * (per_step // piece) + n

            def pair(i):
                got = lag_pair(n * piece + 2 * i)
                for r in range(2):
                    value = got[:, r * chans:(r + 1) * chans]
                    if v < sends:
                        send[v, 2 * i + r] = value.astype(jnp.bfloat16)
                    else:
                        own[(v - sends) * piece + 2 * i + r] = value

            repeat(piece // 2, min(2, piece // 2), pair)
            if v < sends:
                exchange(v).start()

    def close(w):
        for p in range(1, peers):
            exchange((p - 1) * (block // piece) + w).wait()

        def one(j):
            value = own[w * piece + j]
            for p in range(1, peers):
                value = value + recv[(p - 1) * (block // piece) + w, j].astype(jnp.float32)
            out_ref[w * piece + j] = value.T

        repeat(piece, 2, one)

    parts_of = 2 + per_step // piece
    urgent = -(-sends // (per_step // piece))
    wait_of = [1.6 if d == 1 else 3.2 if d < 8 else 5.2 for d in stages]
    now, ready, stage_of = 0.0, {}, {}
    done = [0] * steps
    later = []
    for t in range(steps):
        if t < max(urgent, 1):
            copy(t, 0).start()
            ready[t], stage_of[t] = wait_of[0] * (t + 1), 0
        else:
            later.append(t)
    while any(n < parts_of for n in done):
        if later and now >= sum(wait_of[:3]):
            for t in later:
                copy(t, 0).start()
                ready[t], stage_of[t] = now + wait_of[0] * (t + 1 - later[0]), 0
            later = []
        due = [t for t in ready if ready[t] <= now]
        todo = [t for t in range(steps) if stage_of.get(t) == len(stages) and done[t] < parts_of]
        if not due and todo:
            compute(todo[0], done[todo[0]])
            now += 2.2 if done[todo[0]] < 2 else 0.7
            done[todo[0]] += 1
        else:
            t = due[0] if due else min(ready, key=lambda i: ready[i])
            now = max(now, ready[t])
            finish(t, stage_of[t])
            stage_of[t] += 1
            if stage_of[t] < len(stages):
                copy(t, stage_of[t]).start()
                ready[t] = now + wait_of[stage_of[t]]
            else:
                del ready[t]
    for w in range(block // piece):
        close(w)


def per_device(spectra, owners, source_rows):
    _, bins, wins, chans = spectra.shape
    steps, per_step = source_rows.shape
    n_chan, n_tm, n_freq = (lax.axis_size(a) for a in AXES[1:])
    peers = n_tm * n_freq
    per = per_step // peers
    lanes = bins * wins
    full = jnp.asarray(table(bins * n_freq, 1.0 / (wins * n_tm)).astype(jnp.bfloat16))
    tables = lax.dynamic_slice_in_dim(full, lax.axis_index("freq") * bins, bins, 2) if n_freq > 1 else full
    tables = tables.reshape(LAGS, 2 * bins)
    far = max(n_chan.bit_length() - 3, 1)
    count = n_chan.bit_length() + 1
    sizes = (steps, per_step, bins, wins, chans, n_chan, n_tm, n_freq)
    bf16, f32 = jnp.bfloat16, jnp.float32
    quarter = (per_step, lanes // 2)
    vmem = pl.BlockSpec(memory_space=pltpu.VMEM)
    smem = pl.BlockSpec(memory_space=pltpu.SMEM)
    block, piece, sends = layout(steps, per_step, peers)
    out = pl.pallas_call(
        functools.partial(kernel, sizes),
        out_shape=jax.ShapeDtypeStruct((block, chans, LAGS), f32),
        in_specs=[smem, smem, vmem, vmem],
        out_specs=vmem,
        scratch_shapes=[
            pltpu.VMEM((steps * per_step, chans), f32),
            pltpu.VMEM((lanes // 128, 256, 2 * chans), bf16),
            pltpu.VMEM((steps, 4) + quarter, bf16),
            pltpu.VMEM((steps, 2) + quarter, bf16),
            pltpu.VMEM((steps,) + quarter, bf16),
            pltpu.VMEM((steps, far) + quarter, bf16),
            pltpu.VMEM((steps, 4) + quarter, bf16),
            pltpu.VMEM((per_step, 2 * bins, chans), bf16),
            pltpu.VMEM((block, LAGS, chans), f32),
            pltpu.VMEM((max(sends, 1), piece, LAGS, chans), bf16),
            pltpu.VMEM((max(sends, 1), piece, LAGS, chans), bf16),
            pltpu.SemaphoreType.DMA((steps, count)),
            pltpu.SemaphoreType.DMA((steps, count)),
            pltpu.SemaphoreType.DMA((max(sends, 1),)),
            pltpu.SemaphoreType.DMA((max(sends, 1),)),
        ],
        compiler_params=pltpu.CompilerParams(collective_id=0, has_side_effects=True),
    )(owners, source_rows, spectra.reshape(2, lanes, chans), tables)
    return out.reshape(steps, per, chans, LAGS)


def solution(mesh):
    placed = (P(None, "freq", "tm", ("parts", "chan")), P("parts"), P("parts", None))
    return jax.shard_map(
        per_device,
        mesh=mesh,
        in_specs=placed,
        out_specs=P(None, ("tm", "freq"), ("parts", "chan"), None),
        check_vma=False,
    )
```

```python
import functools

import jax
import jax.numpy as jnp
import numpy as np
from jax import lax
from jax.experimental import pallas as pl
from jax.experimental.pallas import tpu as pltpu
from jax.sharding import PartitionSpec as P

WINDOW_LEN = 4096
FIRST_BIN = 64
LAGS = 128
WATER = 0.5
AXES = ("parts", "chan", "tm", "freq")
MESH = pl.DeviceIdType.MESH


def table(count, scale):
    bins = FIRST_BIN + np.arange(count)
    shifts = np.arange(LAGS) - LAGS // 2
    angle = np.mod(shifts[:, None] * bins[None, :], WINDOW_LEN) * (2.0 * np.pi / WINDOW_LEN)
    return np.stack([np.cos(angle), -np.sin(angle)], axis=1) * scale


def layout(steps, per_step, peers):
    block = steps * (per_step // peers)
    piece = max(min(per_step, block) // 2, 2)
    return block, piece, (peers - 1) * block // piece


def kernel(sizes, owner_ref, row_ref, spec_ref, table_ref, out_ref,
           pick, right, held, got1, got2, got_full, whole, cross, own, send, recv,
           bsend, brecv, xsend, xrecv):
    steps, per_step, bins, wins, chans, n_chan, n_tm, n_freq = sizes
    group = 128 // wins
    lanes = bins * wins
    half = lanes // 2
    groups = lanes // 128
    peers = n_tm * n_freq
    per = per_step // peers
    block, piece, sends = layout(steps, per_step, peers)
    part, me = lax.axis_index("parts"), lax.axis_index("chan")
    tm, fq = lax.axis_index("tm"), lax.axis_index("freq")
    rank = tm * n_freq + fq
    bit0, bit1 = me % 2, (me // 2) % 2
    dists = []
    while 2 ** len(dists) < n_chan:
        dists.append(2 ** len(dists))
    far = dists[2:]
    stages = [1, 2] + far + [2, 1]

    def along(d):
        return (part, me + d * (1 - 2 * ((me // d) % 2)), tm, fq)

    def peer(p):
        other = (rank + p) % peers
        return (part, me, other // n_freq, other % n_freq)

    barrier = pltpu.get_barrier_semaphore()
    for d in dists:
        pl.semaphore_signal(barrier, inc=1, device_id=along(d), device_id_type=MESH)
    for p in range(1, peers):
        pl.semaphore_signal(barrier, inc=1, device_id=peer(p), device_id_type=MESH)

    channel = lax.broadcasted_iota(jnp.int32, (1, chans), 1)
    for p in range(1, peers + 1):
        for t in range(steps):
            held_here = owner_ref[t] == me
            for j in range(per):
                row = jnp.where(held_here, row_ref[t, ((rank + p) % peers) * per + j], -1)
                at = (p - 1) * block + t * per + j
                pick[pl.ds(at, 1), :] = (channel == row).astype(jnp.float32)
    chosen = pick[...].astype(jnp.bfloat16)

    def prepare(h, i):
        g = h * (groups // 2) + i
        at = pl.ds(pl.multiple_of(g * 128, 128), 128)
        re = spec_ref[0, at, :].astype(jnp.float32)
        im = spec_ref[1, at, :].astype(jnp.float32)
        inverse = 1.0 / (jnp.sqrt(re * re + im * im) + WATER)
        re = (re * inverse).astype(jnp.bfloat16)
        im = (im * inverse).astype(jnp.bfloat16)
        right[g, :128, :chans] = re
        right[g, :128, chans:] = im
        right[g, 128:, :chans] = im
        right[g, 128:, chans:] = -re
        both = jnp.concatenate([re, im], axis=0)
        got = lax.dot_general(chosen, both, (((1,), (1,)), ((), ())),
                              preferred_element_type=jnp.float32).astype(jnp.bfloat16)
        to = pl.ds(pl.multiple_of(i * 128, 128), 128)
        for u in range(steps):
            for k in range(2):
                held[u, 2 * k + h, :, to] = got[u * per_step:(u + 1) * per_step, k * 128:(k + 1) * 128]

    def repeat(count, unroll, body):
        def some(i, carry):
            for r in range(unroll):
                body(i * unroll + r)
            return carry

        lax.fori_loop(0, count // unroll, some, 0)

    for h in range(2):
        repeat(groups // 2, 4, functools.partial(prepare, h))

    pl.semaphore_wait(barrier, len(dists) + peers - 1)

    keep = 2 * bit0 + bit1
    last = len(stages) - 1

    def copy(t, st):
        d = stages[st]
        if st == 0:
            src, dst = held.at[t, pl.ds(2 * (1 - bit0), 2)], got1.at[t]
        elif st == 1:
            src, dst = held.at[t, 2 * bit0 + 1 - bit1], got2.at[t]
        elif st < last - 1:
            src, dst = held.at[t, keep], got_full.at[t, st - 2]
        elif st == last - 1:
            src = dst = whole.at[t, keep]
        else:
            src = dst = whole.at[t, pl.ds(2 * bit0, 2)]
        return pltpu.make_async_remote_copy(
            src_ref=src, dst_ref=dst, send_sem=bsend.at[t, st], recv_sem=brecv.at[t, st],
            device_id=along(d), device_id_type=MESH)

    def finish(t, st):
        copy(t, st).wait()
        if st == 0:
            for q in range(2):
                held[t, 2 * bit0 + q] = held[t, 2 * bit0 + q] + got1[t, q]
        elif st == 1:
            held[t, keep] = held[t, keep] + got2[t]
        elif st < last - 1:
            held[t, keep] = held[t, keep] + got_full[t, st - 2]
        if st == last - 2:
            whole[t, keep] = held[t, keep]

    lane = lax.broadcasted_iota(jnp.int32, (1, group, 128), 2)
    bin_of = lax.broadcasted_iota(jnp.int32, (1, group, 128), 1)
    mine = (lane // wins) == bin_of

    def spread(x):
        wide = jnp.where(mine, x[:, None, :], 0.0)
        return wide.reshape(per_step * group, 128).astype(jnp.bfloat16)

    def exchange(v):
        return pltpu.make_async_remote_copy(
            src_ref=send.at[v], dst_ref=recv.at[v], send_sem=xsend.at[v], recv_sem=xrecv.at[v],
            device_id=peer(v * piece // block + 1), device_id_type=MESH)

    def multiply(u, h):
        def one(i):
            g = pl.multiple_of(i * 128, 128)
            re = whole[u, h, :, pl.ds(g, 128)].astype(jnp.float32)
            im = whole[u, 2 + h, :, pl.ds(g, 128)].astype(jnp.float32)
            left = jnp.concatenate([spread(re), spread(im)], axis=1)
            got = jnp.dot(left, right[h * (groups // 2) + i], preferred_element_type=jnp.float32)
            first = h * (bins // 2) + i * group
            for o in range(2):
                to = pl.ds(pl.multiple_of(o * bins + first, group), group)
                value = got[:, o * chans:(o + 1) * chans]
                cross[:, to, :] = value.reshape(per_step, group, chans).astype(jnp.bfloat16)

        repeat(groups // 2, 2, one)

    def lag_pair(s):
        both = jnp.concatenate([cross[s], cross[s + 1]], axis=1)
        return jnp.dot(table_ref[...], both, preferred_element_type=jnp.float32)

    def compute(u, part_of):
        if part_of < 2:
            multiply(u, part_of)
        else:
            n = part_of - 2
            v = u * (per_step // piece) + n

            def pair(i):
                got = lag_pair(n * piece + 2 * i)
                for r in range(2):
                    value = got[:, r * chans:(r + 1) * chans]
                    if v < sends:
                        send[v, 2 * i + r] = value.astype(jnp.bfloat16)
                    else:
                        own[(v - sends) * piece + 2 * i + r] = value

            repeat(piece // 2, min(2, piece // 2), pair)
            if v < sends:
                exchange(v).start()

    def close(w):
        for p in range(1, peers):
            exchange((p - 1) * (block // piece) + w).wait()

        def one(j):
            value = own[w * piece + j]
            for p in range(1, peers):
                value = value + recv[(p - 1) * (block // piece) + w, j].astype(jnp.float32)
            out_ref[w * piece + j] = value.T

        repeat(piece, 2, one)

    parts_of = 2 + per_step // piece
    wait_of = [1.6 if d == 1 else 3.2 if d < 8 else 5.2 for d in stages]
    now, ready, stage_of = 0.0, {}, {}
    done = [0] * steps
    for t in range(steps):
        copy(t, 0).start()
        ready[t], stage_of[t] = wait_of[0] * (t + 1), 0
    while any(n < parts_of for n in done):
        due = [t for t in ready if ready[t] <= now]
        todo = [t for t in range(steps) if stage_of.get(t) == len(stages) and done[t] < parts_of]
        if not due and todo:
            compute(todo[0], done[todo[0]])
            now += 2.2 if done[todo[0]] < 2 else 0.7
            done[todo[0]] += 1
        else:
            t = due[0] if due else min(ready, key=lambda i: ready[i])
            now = max(now, ready[t])
            finish(t, stage_of[t])
            stage_of[t] += 1
            if stage_of[t] < len(stages):
                copy(t, stage_of[t]).start()
                ready[t] = now + wait_of[stage_of[t]]
            else:
                del ready[t]
    for w in range(block // piece):
        close(w)


def per_device(spectra, owners, source_rows):
    _, bins, wins, chans = spectra.shape
    steps, per_step = source_rows.shape
    n_chan, n_tm, n_freq = (lax.axis_size(a) for a in AXES[1:])
    peers = n_tm * n_freq
    per = per_step // peers
    lanes = bins * wins
    full = jnp.asarray(table(bins * n_freq, 1.0 / (wins * n_tm)).astype(jnp.bfloat16))
    tables = lax.dynamic_slice_in_dim(full, lax.axis_index("freq") * bins, bins, 2) if n_freq > 1 else full
    tables = tables.reshape(LAGS, 2 * bins)
    far = max(n_chan.bit_length() - 3, 1)
    count = n_chan.bit_length() + 1
    sizes = (steps, per_step, bins, wins, chans, n_chan, n_tm, n_freq)
    bf16, f32 = jnp.bfloat16, jnp.float32
    quarter = (per_step, lanes // 2)
    vmem = pl.BlockSpec(memory_space=pltpu.VMEM)
    smem = pl.BlockSpec(memory_space=pltpu.SMEM)
    block, piece, sends = layout(steps, per_step, peers)
    out = pl.pallas_call(
        functools.partial(kernel, sizes),
        out_shape=jax.ShapeDtypeStruct((block, chans, LAGS), f32),
        in_specs=[smem, smem, vmem, vmem],
        out_specs=vmem,
        scratch_shapes=[
            pltpu.VMEM((steps * per_step, chans), f32),
            pltpu.VMEM((lanes // 128, 256, 2 * chans), bf16),
            pltpu.VMEM((steps, 4) + quarter, bf16),
            pltpu.VMEM((steps, 2) + quarter, bf16),
            pltpu.VMEM((steps,) + quarter, bf16),
            pltpu.VMEM((steps, far) + quarter, bf16),
            pltpu.VMEM((steps, 4) + quarter, bf16),
            pltpu.VMEM((per_step, 2 * bins, chans), bf16),
            pltpu.VMEM((block, LAGS, chans), f32),
            pltpu.VMEM((max(sends, 1), piece, LAGS, chans), bf16),
            pltpu.VMEM((max(sends, 1), piece, LAGS, chans), bf16),
            pltpu.SemaphoreType.DMA((steps, count)),
            pltpu.SemaphoreType.DMA((steps, count)),
            pltpu.SemaphoreType.DMA((max(sends, 1),)),
            pltpu.SemaphoreType.DMA((max(sends, 1),)),
        ],
        compiler_params=pltpu.CompilerParams(collective_id=0, has_side_effects=True),
    )(owners, source_rows, spectra.reshape(2, lanes, chans), tables)
    return out.reshape(steps, per, chans, LAGS)


def solution(mesh):
    placed = (P(None, "freq", "tm", ("parts", "chan")), P("parts"), P("parts", None))
    return jax.shard_map(
        per_device,
        mesh=mesh,
        in_specs=placed,
        out_specs=P(None, ("tm", "freq"), ("parts", "chan"), None),
        check_vma=False,
    )
```
